32 devices in a mesh: ctx: 8 (over y, x, core), tp: 4 (over z).
Axes of the slice: x: 2, y: 2, z: 4, core: 2. Of those that a mesh axis runs over, the one named last changes fastest.
Arguments:
- queries: bfloat16 [2048, 4096], P('ctx', 'tp'), may hold values from -6 to 6
- attn_keys: bfloat16 [2048, 4096], P('ctx', 'tp'), may hold values from -6 to 6
- attn_values: bfloat16 [2048, 4096], P('ctx', 'tp'), may hold values from -6 to 6
- out_proj: bfloat16 [4096, 8192], P('tp'), may hold values from -0.25 to 0.25
Outputs:
- mixed: bfloat16 [2048, 8192], P('ctx', 'tp')
The draws below stay inside these ranges and needn't reach their ends.
All inputs are finite; a program needn't handle non-finite values.
Results may differ from the reference program's by a relative error of at most 0.013.
Values may be sent and summed in bfloat16 or wider, within the bound.
No kernel may reach another device: no remote copies, remote signals or barrier semaphores. Data moves between devices by JAX's collectives and lax.ppermute only.
A program may use at most 256 MiB of HBM per device.

```python
import jax
import jax.numpy as jnp
from jax import lax

D = 8192
HEADS = 32
HS = 128
HALF = 128
SEQ = 2048
INNER = 4096
N_CTX = 8
N_TP = 4


def draw_queries(key, part):
    base_key = jax.random.fold_in(key, 11)
    values = jnp.clip(1.6 * jax.random.normal(base_key, (SEQ, HEADS * HS), jnp.float32), -6.0, 6.0)
    return values.astype(jnp.bfloat16)


def draw_attn_keys(key, part):
    base_key = jax.random.fold_in(key, 13)
    values = jnp.clip(1.6 * jax.random.normal(base_key, (SEQ, HEADS * HS), jnp.float32), -6.0, 6.0)
    return values.astype(jnp.bfloat16)


def block_levels(stream_key, dims, cuts, smallest, high):
    factor_of, own = 1.0, jax.random.fold_in(stream_key, 6)
    for axis_at, blocks in cuts:
        draws = jnp.exp(jax.random.uniform(jax.random.fold_in(own, axis_at), (blocks,), jnp.float32, smallest / len(cuts), high / len(cuts)))
        factor_of = factor_of * jnp.repeat(draws, dims[axis_at] // blocks).reshape([-1 if axis == axis_at else 1 for axis in range(len(dims))])
    return factor_of


def scatter_about(own_key, dims, spread, most, split=(), kind=jnp.bfloat16):
    factor_of = block_levels(own_key, dims, split, -0.22, 0.18) if split else 1.0
    values = jax.random.normal(own_key, dims, jnp.float32) * spread * factor_of
    return jnp.minimum(jnp.maximum(values, -most), most).astype(kind)


def setup_inputs(seed: int = 0) -> dict:
    key_of = jax.random.split(jax.random.key(seed), 5)
    return {
        "queries": draw_queries(jax.random.fold_in(key_of[4], 71), 0),
        "attn_keys": draw_attn_keys(jax.random.fold_in(key_of[4], 71), 0),
        "attn_values": scatter_about(key_of[2], (SEQ, INNER), 1.0, 6.0, ((0, 8), (1, 4))),
        "out_proj": scatter_about(key_of[3], (INNER, D), (INNER // 9) ** -0.5, 0.25, ((0, 4),)),
    }


def block_order():
    blocks = jnp.arange(2 * N_CTX, dtype=jnp.int32)
    device = blocks // 2
    seq_block = jnp.where(blocks % 2 == 0, device, 2 * N_CTX - 1 - device).astype(jnp.int32)
    return seq_block


def reference(queries, attn_keys, attn_values, out_proj):
    seq_block = block_order()
    position = (seq_block[:, None] * HALF + jnp.arange(HALF, dtype=jnp.int32)[None, :]).reshape(-1).astype(jnp.int32)
    scale = 1.0 / (HS ** 0.5)
    visible = position[None, :] <= position[:, None]

    def one_head(operands):
        query_head, key_head, value_head = operands
        scores = jnp.dot(query_head.astype(jnp.float32), key_head.astype(jnp.float32).T,
                         precision=lax.Precision.HIGHEST) * scale
        top = jnp.max(jnp.where(visible, scores, -jnp.inf), axis=1, keepdims=True)
        weights = jnp.where(visible, jnp.exp(scores - top), 0.0)
        total = jnp.sum(weights, axis=1, keepdims=True)
        rounded = weights.astype(jnp.bfloat16).astype(jnp.float32)
        return jnp.dot(rounded, value_head.astype(jnp.float32), precision=lax.Precision.HIGHEST) / total

    def by_heads(array):
        return jnp.transpose(array.reshape(SEQ, HEADS, HS), (1, 0, 2))

    attended = lax.map(one_head, (by_heads(queries), by_heads(attn_keys), by_heads(attn_values)))
    attended = jnp.transpose(attended, (1, 0, 2)).reshape(SEQ, HEADS * HS).astype(jnp.bfloat16)
    group_cols = HEADS * HS // N_TP
    mixed = jnp.zeros((SEQ, out_proj.shape[1]), jnp.float32)
    for group in range(N_TP):
        part_cols = attended[:, group * group_cols:(group + 1) * group_cols]
        part_rows = out_proj[group * group_cols:(group + 1) * group_cols]
        partial_value = jnp.dot(part_cols, part_rows, preferred_element_type=jnp.float32).astype(jnp.bfloat16)
        mixed = mixed + partial_value.astype(jnp.float32)
    return mixed.astype(jnp.bfloat16)
```

```python
import functools
import math

import jax
import jax.numpy as jnp
from jax import lax
from jax.experimental import pallas as pl
from jax.experimental.pallas import tpu as pltpu
from jax.sharding import PartitionSpec as P

HS = 128
ANY = pl.BlockSpec(memory_space=pl.ANY)
PARAMS = pltpu.CompilerParams(vmem_limit_bytes=16 << 20)


def gathered_attention(queries, attn_keys, attn_values):
    ctx_count = lax.axis_size("ctx")
    ctx_index = lax.axis_index("ctx")
    tok_dev = queries.shape[0]
    half_len = tok_dev // 2
    heads_local = queries.shape[1] // HS
    query_heads = queries.reshape(tok_dev, heads_local, HS)
    offsets = jnp.arange(half_len, dtype=jnp.int32)
    query_pos = jnp.concatenate(
        [ctx_index * half_len + offsets, (2 * ctx_count - 1 - ctx_index) * half_len + offsets]
    )
    key_heads = lax.all_gather(attn_keys, "ctx", axis=0, tiled=True).reshape(-1, heads_local, HS)
    value_heads = lax.all_gather(attn_values, "ctx", axis=0, tiled=True).reshape(-1, heads_local, HS)
    stored = jnp.arange(key_heads.shape[0], dtype=jnp.int32)
    device = stored // tok_dev
    within = stored % tok_dev
    key_pos = jnp.where(
        within < half_len,
        device * half_len + within,
        (2 * ctx_count - 1 - device) * half_len + within - half_len,
    )
    scores = jnp.einsum("rhd,phd->hrp", query_heads, key_heads, preferred_element_type=jnp.float32)
    scores = scores * (1.0 / HS**0.5)
    visible = key_pos[None, None, :] <= query_pos[None, :, None]
    scores = jnp.where(visible, scores, -1e30)
    top = jnp.max(scores, axis=2, keepdims=True)
    weights = jnp.where(visible, jnp.exp(scores - top), 0.0)
    total = jnp.sum(weights, axis=2)
    update = jnp.einsum(
        "hrp,phd->rhd", weights.astype(jnp.bfloat16), value_heads, preferred_element_type=jnp.float32
    )
    attended = update / jnp.transpose(total)[:, :, None]
    return attended.reshape(tok_dev, heads_local * HS).astype(jnp.bfloat16)


def general_body(queries, attn_keys, attn_values, out_proj):
    attended = gathered_attention(queries, attn_keys, attn_values)
    partial_value = jnp.dot(attended, out_proj, preferred_element_type=jnp.float32).astype(
        jnp.bfloat16
    )
    return lax.psum_scatter(partial_value, "tp", scatter_dimension=1, tiled=True)


def pack_kernel(row0, q_ref, k_ref, v_ref, *rest):
    outs, sems = rest[:-1], rest[-1]
    half, width = outs[0].shape[1:]
    group = lax.axis_index("ctx") // 2
    copies = []
    for j, out in enumerate(outs):
        column = pl.multiple_of(lax.bitwise_xor(group, j) * width, width)
        for i, ref in enumerate((q_ref, k_ref, v_ref)):
            copy = pltpu.make_async_copy(
                ref.at[pl.ds(row0, half), pl.ds(column, width)], out.at[i], sems.at[3 * j + i]
            )
            copy.start()
            copies.append(copy)
    for copy in copies:
        copy.wait()


def pack(queries, attn_keys, attn_values, row0, half, groups):
    width = queries.shape[1] // groups
    out = jax.ShapeDtypeStruct((3, half, width), queries.dtype)
    return pl.pallas_call(
        functools.partial(pack_kernel, row0),
        out_shape=[out] * groups,
        in_specs=[ANY] * 3,
        out_specs=[ANY] * groups,
        scratch_shapes=[pltpu.SemaphoreType.DMA((3 * groups,))],
        name="pack",
        compiler_params=PARAMS,
        cost_estimate=pl.CostEstimate(
            flops=0, bytes_accessed=6 * half * width * groups * 2, transcendentals=0
        ),
    )(queries, attn_keys, attn_values)


def softmax_rows(pieces):
    rate = math.log2(math.e) / HS**0.5
    top = None
    for scores, _ in pieces:
        here = jnp.max(scores, axis=1, keepdims=True)
        top = here if top is None else jnp.maximum(top, here)
    total, acc = None, None
    for scores, values in pieces:
        weights = jnp.exp2((scores - top) * rate)
        add = jnp.sum(weights, axis=1, keepdims=True)
        dot = jnp.dot(weights.astype(jnp.bfloat16), values, preferred_element_type=jnp.float32)
        total = add if total is None else total + add
        acc = dot if acc is None else acc + dot
    return acc / total


def attention_kernel(groups, phases, *refs):
    per_phase = groups + 1
    ins = refs[: phases * per_phase]
    outs = refs[phases * per_phase : phases * per_phase + groups]
    q_s, k_s, v_s, o_s, in_sems, out_sems = refs[phases * per_phase + groups :]
    half, width = outs[0].shape
    index = lax.axis_index("ctx")
    group, core = index // 2, lax.rem(index, 2)
    copies = []

    def start(src, dst):
        copy = pltpu.make_async_copy(src, dst, in_sems.at[len(copies)])
        copy.start()
        copies.append(copy)

    for phase in range(phases):
        own = ins[phase * per_phase : phase * per_phase + groups]
        other = ins[phase * per_phase + groups]
        for j in range(groups):
            at = lax.bitwise_xor(group, j)
            if phase == phases - 1:
                start(own[j].at[0], q_s.at[at])
            start(own[j].at[1], k_s.at[phase, at, core])
            start(own[j].at[2], v_s.at[phase, at, core])
            start(other.at[j, 0], k_s.at[phase, at, 1 - core])
            start(other.at[j, 1], v_s.at[phase, at, 1 - core])
    for copy in copies:
        copy.wait()

    sign = 1 if phases == 1 else -1
    row = lax.broadcasted_iota(jnp.int32, (half, 2 * half), 0)
    col = lax.broadcasted_iota(jnp.int32, (half, 2 * half), 1)
    block, within = col // half, col % half
    visible = sign * half * block + within <= sign * half * core + row
    contract = (((1,), (1,)), ((), ()))

    for head in range(width // HS):
        lanes = slice(head * HS, (head + 1) * HS)
        for at in range(groups):
            query = q_s[at][:, lanes]
            pieces = []

            def add(phase, lo, hi, masked):
                if lo >= hi:
                    return
                keys = k_s[phase, lo:hi][:, :, :, lanes].reshape(-1, HS)
                values = v_s[phase, lo:hi][:, :, :, lanes].reshape(-1, HS)
                scores = lax.dot_general(query, keys, contract, preferred_element_type=jnp.float32)
                if masked:
                    scores = jnp.where(visible, scores, -1e30)
                pieces.append((scores, values))

            if phases == 1:
                add(0, 0, at, False)
                add(0, at, at + 1, True)
            else:
                add(0, 0, groups, False)
                add(1, at + 1, groups, False)
                add(1, at, at + 1, True)
            o_s[at, :, lanes] = softmax_rows(pieces).astype(o_s.dtype)

    copies = []
    for j in range(groups):
        copy = pltpu.make_async_copy(o_s.at[lax.bitwise_xor(group, j)], outs[j], out_sems.at[j])
        copy.start()
        copies.append(copy)
    for copy in copies:
        copy.wait()


def attention(phase_inputs, groups, half, width):
    phases = len(phase_inputs)
    flat = [array for own, other in phase_inputs for array in (*own, other)]
    out = jax.ShapeDtypeStruct((half, width), jnp.bfloat16)
    n_in = groups + phases * groups * 4
    elements = groups * width // HS * half * half * (groups + 1 if phases == 1 else 3 * groups + 1)
    return pl.pallas_call(
        functools.partial(attention_kernel, groups, phases),
        out_shape=[out] * groups,
        in_specs=[ANY] * len(flat),
        out_specs=[ANY] * groups,
        scratch_shapes=[
            pltpu.VMEM((groups, half, width), jnp.bfloat16),
            pltpu.VMEM((phases, groups, 2, half, width), jnp.bfloat16),
            pltpu.VMEM((phases, groups, 2, half, width), jnp.bfloat16),
            pltpu.VMEM((groups, half, width), jnp.bfloat16),
            pltpu.SemaphoreType.DMA((n_in,)),
            pltpu.SemaphoreType.DMA((groups,)),
        ],
        name=f"attention{phases}",
        compiler_params=PARAMS,
        cost_estimate=pl.CostEstimate(
            flops=4 * HS * elements, bytes_accessed=2 << 20, transcendentals=elements
        ),
    )(*flat)


def project_kernel(groups, place_ref, *refs):
    ins, w_ref, out_ref = refs[:groups], refs[groups], refs[-1]
    depth = ins[0].shape[1]
    acc = None
    for j in range(groups):
        at = pl.multiple_of(lax.bitwise_xor(place_ref[1], j) * depth, depth)
        dot = jnp.dot(ins[j][...], w_ref[pl.ds(at, depth), :], preferred_element_type=jnp.float32)
        acc = dot if acc is None else acc + dot
    out_ref[...] = acc.astype(out_ref.dtype)


def project(parts, out_proj, target, group, tp_count, dtype):
    groups = len(parts)
    half, depth = parts[0].shape
    columns = out_proj.shape[1] // tp_count
    tile = columns // 4 if columns % 512 == 0 else columns
    tiles = columns // tile
    place = jnp.stack([target, group]).astype(jnp.int32)
    grid_spec = pltpu.PrefetchScalarGridSpec(
        num_scalar_prefetch=1,
        grid=(tiles,),
        in_specs=[pl.BlockSpec((half, depth), lambda i, place: (0, 0))] * groups
        + [pl.BlockSpec((out_proj.shape[0], tile), lambda i, place: (0, place[0] * tiles + i))],
        out_specs=pl.BlockSpec((half, tile), lambda i, place: (0, i)),
    )
    return pl.pallas_call(
        functools.partial(project_kernel, groups),
        out_shape=jax.ShapeDtypeStruct((half, columns), dtype),
        grid_spec=grid_spec,
        name="project",
        compiler_params=PARAMS,
        cost_estimate=pl.CostEstimate(
            flops=2 * half * out_proj.shape[0] * columns,
            bytes_accessed=2 * out_proj.shape[0] * columns,
            transcendentals=0,
        ),
    )(place, *parts, out_proj)


def exchange_body(queries, attn_keys, attn_values, out_proj):
    ctx_count, tp_count = lax.axis_size("ctx"), lax.axis_size("tp")
    group = lax.axis_index("ctx") // 2
    z = lax.axis_index("tp")
    groups = ctx_count // 2
    half = queries.shape[0] // 2
    width = queries.shape[1] // groups
    f32, bf16 = jnp.float32, jnp.bfloat16

    def swap(array, j):
        return lax.ppermute(array, "ctx", [(d, d ^ (2 * j)) for d in range(ctx_count)])

    def pair_swap(array):
        return lax.ppermute(array, "ctx", [(d, d ^ 1) for d in range(ctx_count)])

    def tokens(row0):
        packed = pack(queries, attn_keys, attn_values, row0, half, groups)
        return [packed[0]] + [swap(packed[j], j) for j in range(1, groups)]

    def paired(own):
        return own, pair_swap(jnp.stack([array[1:] for array in own]))

    def back(outs):
        return [outs[0]] + [swap(outs[j], j) for j in range(1, groups)]

    low = paired(tokens(0))
    high = tokens(half)
    parts_low = back(attention([low], groups, half, width))
    high, parts_low = lax.optimization_barrier((high, parts_low))
    high = paired(high)
    parts_high = back(attention([low, high], groups, half, width))

    def line(parts):
        def chunk(target, dtype=f32):
            target = jnp.clip(target, 0, tp_count - 1)
            return project(parts, out_proj, target, group, tp_count, dtype)

        def add(mine, arrived):
            for array in arrived:
                if array is not None:
                    mine = mine + array.astype(f32)
            return mine.astype(bf16)

        right, left = None, None
        for step in range(1, tp_count):
            far = tp_count - step
            to_right = [(i, i + 1) for i in range(step)]
            to_left = [(i, i - 1) for i in range(far, tp_count)]
            if step <= far:
                mine = chunk(jnp.where(z < step, z + far, z - far))
                send = add(mine, (right, left))
                send_right = send_left = send
            else:
                send_right = add(chunk(z + far), (right,))
                send_left = add(chunk(z - far), (left,))
            right = lax.ppermute(send_right, "tp", to_right)
            left = lax.ppermute(send_left, "tp", to_left)
        return add(chunk(z), (right, left))

    return jnp.concatenate([line(parts_low), line(parts_high)], axis=0)


def body(queries, attn_keys, attn_values, out_proj):
    ctx_count = lax.axis_size("ctx")
    heads_local = queries.shape[1] // HS
    groups = ctx_count // 2
    paired = ctx_count % 2 == 0 and groups >= 1 and groups & (groups - 1) == 0
    if paired and heads_local % groups == 0:
        return exchange_body(queries, attn_keys, attn_values, out_proj)
    return general_body(queries, attn_keys, attn_values, out_proj)


def solution(mesh):
    in_specs = (P("ctx", "tp"), P("ctx", "tp"), P("ctx", "tp"), P("tp", None))
    out_specs = P("ctx", "tp")
    return jax.shard_map(body, mesh=mesh, in_specs=in_specs, out_specs=out_specs, check_vma=False)
```

```python
import functools
import math

import jax
import jax.numpy as jnp
from jax import lax
from jax.experimental import pallas as pl
from jax.experimental.pallas import tpu as pltpu
from jax.sharding import PartitionSpec as P


HS = 128
ANY = pl.BlockSpec(memory_space=pl.ANY)
HBM = pl.BlockSpec(memory_space=pltpu.HBM)
VMEM = pl.BlockSpec(memory_space=pltpu.VMEM)
COPIES = pltpu.CompilerParams(vmem_limit_bytes=1 << 20)
PARAMS = pltpu.CompilerParams(vmem_limit_bytes=8 << 20)


def gathered_attention(queries, attn_keys, attn_values):
    ctx_count = lax.axis_size("ctx")
    ctx_index = lax.axis_index("ctx")
    tok_dev = queries.shape[0]
    half_len = tok_dev // 2
    heads_local = queries.shape[1] // HS
    query_heads = queries.reshape(tok_dev, heads_local, HS)
    offsets = jnp.arange(half_len, dtype=jnp.int32)
    query_pos = jnp.concatenate(
        [ctx_index * half_len + offsets, (2 * ctx_count - 1 - ctx_index) * half_len + offsets]
    )
    key_heads = lax.all_gather(attn_keys, "ctx", axis=0, tiled=True).reshape(-1, heads_local, HS)
    value_heads = lax.all_gather(attn_values, "ctx", axis=0, tiled=True).reshape(-1, heads_local, HS)
    stored = jnp.arange(key_heads.shape[0], dtype=jnp.int32)
    device = stored // tok_dev
    within = stored % tok_dev
    key_pos = jnp.where(
        within < half_len,
        device * half_len + within,
        (2 * ctx_count - 1 - device) * half_len + within - half_len,
    )
    scores = jnp.einsum("rhd,phd->hrp", query_heads, key_heads, preferred_element_type=jnp.float32)
    scores = scores * (1.0 / HS**0.5)
    visible = key_pos[None, None, :] <= query_pos[None, :, None]
    scores = jnp.where(visible, scores, -1e30)
    top = jnp.max(scores, axis=2, keepdims=True)
    weights = jnp.where(visible, jnp.exp(scores - top), 0.0)
    total = jnp.sum(weights, axis=2)
    update = jnp.einsum(
        "hrp,phd->rhd", weights.astype(jnp.bfloat16), value_heads, preferred_element_type=jnp.float32
    )
    attended = update / jnp.transpose(total)[:, :, None]
    return attended.reshape(tok_dev, heads_local * HS).astype(jnp.bfloat16)


def general_body(queries, attn_keys, attn_values, out_proj):
    attended = gathered_attention(queries, attn_keys, attn_values)
    partial_value = jnp.dot(attended, out_proj, preferred_element_type=jnp.float32).astype(
        jnp.bfloat16
    )
    return lax.psum_scatter(partial_value, "tp", scatter_dimension=1, tiled=True)


def my_group():
    return lax.axis_index("ctx") // 2


def run_copies(pairs, sems):
    copies = [pltpu.make_async_copy(src, dst, sems.at[i]) for i, (src, dst) in enumerate(pairs)]
    for copy in copies:
        copy.start()
    for copy in copies:
        copy.wait()


def pack_kernel(row0, q_ref, k_ref, v_ref, *rest):
    outs, sems = rest[:-1], rest[-1]
    half, width = outs[0].shape[1:]
    pairs = []
    for j, out in enumerate(outs):
        column = pl.multiple_of(lax.bitwise_xor(my_group(), j) * width, width)
        for i, ref in enumerate((q_ref, k_ref, v_ref)):
            pairs.append((ref.at[pl.ds(row0, half), pl.ds(column, width)], out.at[i]))
    run_copies(pairs, sems)


def pack(queries, attn_keys, attn_values, row0, half, groups):
    width = queries.shape[1] // groups
    out = jax.ShapeDtypeStruct((3, half, width), queries.dtype)
    return pl.pallas_call(
        functools.partial(pack_kernel, row0),
        out_shape=[out] * groups,
        in_specs=[HBM] * 3,
        out_specs=[VMEM] * groups,
        scratch_shapes=[pltpu.SemaphoreType.DMA((3 * groups,))],
        compiler_params=COPIES,
        cost_estimate=pl.CostEstimate(
            flops=0, bytes_accessed=6 * half * width * groups * 2, transcendentals=0
        ),
    )(queries, attn_keys, attn_values)


def piece_kernel(tp_count, w_ref, out_ref, sems):
    width = out_ref.shape[1]
    z = lax.axis_index("tp")
    target = jnp.where(z == 0, 1, tp_count - 2)
    column = target * (w_ref.shape[1] // tp_count) + lax.axis_index("ctx") * width
    column = pl.multiple_of(column, width)
    run_copies([(w_ref.at[:, pl.ds(column, width)], out_ref)], sems)


def piece(out_proj, tp_count, ctx_count):
    width = out_proj.shape[1] // tp_count // ctx_count
    return pl.pallas_call(
        functools.partial(piece_kernel, tp_count),
        out_shape=jax.ShapeDtypeStruct((out_proj.shape[0], width), out_proj.dtype),
        in_specs=[HBM],
        out_specs=VMEM,
        scratch_shapes=[pltpu.SemaphoreType.DMA((1,))],
        name="piece",
        compiler_params=COPIES,
        cost_estimate=pl.CostEstimate(
            flops=0, bytes_accessed=4 * out_proj.shape[0] * width, transcendentals=0
        ),
    )(out_proj)


def attend(groups, phases, group, core, ins, outs):
    half, width = outs[0].shape
    rate = math.log2(math.e) / HS**0.5
    per_phase = groups + 1
    row = lax.broadcasted_iota(jnp.int32, (half, 2 * half), 0)
    col = lax.broadcasted_iota(jnp.int32, (half, 2 * half), 1)
    other_seen = core == (1 if phases == 1 else 0)
    visible = col < jnp.where(other_seen, 2 * half, half)
    visible = visible & ((col >= half) | (col <= row))
    contract = (((1,), (1,)), ((), ()))
    every = list(range(groups))

    tiles = []
    for phase in range(phases):
        for at in every:
            if phase < phases - 1:
                tiles.append((phase, at, every))
            elif phases == 1:
                tiles.append((phase, at, every[at:]))
            else:
                tiles.append((phase, at, every[: at + 1]))

    def keys_of(phase, at, which, lanes):
        own = ins[phase * per_phase + (at ^ group)]
        other = ins[phase * per_phase + groups]
        return jnp.concatenate(
            [own[which, :, lanes], other[at ^ group, which - 1, :, lanes]], axis=0
        )

    def rows(array, i):
        return array[i * half : (i + 1) * half]

    for head in range(width // HS):
        lanes = slice(head * HS, (head + 1) * HS)
        query = {
            at: ins[(phases - 1) * per_phase + (at ^ group)][0, :, lanes] for at in every
        }
        scores, best, total, acc = {}, {}, {}, {}
        for phase, at, seen in tiles:
            tall = jnp.concatenate([query[a] for a in seen], axis=0)
            dot = lax.dot_general(
                tall, keys_of(phase, at, 1, lanes), contract, preferred_element_type=jnp.float32
            )
            for i, a in enumerate(seen):
                mine = rows(dot, i)
                if a == at and phase == phases - 1:
                    mine = jnp.where(visible, mine, -1e30)
                scores[phase, at, a] = mine
                best[a] = jnp.maximum(best[a], mine) if a in best else mine
        top = {a: jnp.max(best[a], axis=1, keepdims=True) for a in every}
        for phase, at, seen in tiles:
            weights = []
            for a in seen:
                mine = jnp.exp2((scores[phase, at, a] - top[a]) * rate)
                total[a] = total[a] + mine if a in total else mine
                weights.append(mine.astype(jnp.bfloat16))
            dot = jnp.dot(
                jnp.concatenate(weights, axis=0),
                keys_of(phase, at, 2, lanes),
                preferred_element_type=jnp.float32,
            )
            for i, a in enumerate(seen):
                mine = rows(dot, i)
                acc[a] = acc[a] + mine if a in acc else mine
        for a in every:
            out = acc[a] / jnp.sum(total[a], axis=1, keepdims=True)
            outs[a ^ group][:, lanes] = out.astype(outs[0].dtype)


def attention_kernel(groups, phases, *refs):
    ins, outs = refs[:-groups], refs[-groups:]
    core = lax.rem(lax.axis_index("ctx"), 2)
    for group in range(groups):

        @pl.when(my_group() == group)
        def _(group=group):
            attend(groups, phases, group, core, ins, outs)


def attention(phase_inputs, groups, half, width):
    phases = len(phase_inputs)
    flat = [array for own, other in phase_inputs for array in (*own, other)]
    out = jax.ShapeDtypeStruct((half, width), jnp.bfloat16)
    elements = groups * width // HS * half * half * (groups + 1 if phases == 1 else 3 * groups + 1)
    return pl.pallas_call(
        functools.partial(attention_kernel, groups, phases),
        out_shape=[out] * groups,
        in_specs=[VMEM] * len(flat),
        out_specs=[VMEM] * groups,
        compiler_params=PARAMS,
        cost_estimate=pl.CostEstimate(
            flops=4 * HS * elements, bytes_accessed=2 << 20, transcendentals=elements
        ),
    )(*flat)


def hold_kernel(place_ref, w_ref, out_ref, sems):
    columns, count = out_ref.shape[1], sems.shape[0]
    rows = out_ref.shape[0] // count
    at = pl.ds(pl.multiple_of(place_ref[0] * columns, columns), columns)
    pairs = []
    for i in range(count):
        band = pl.ds(i * rows, rows)
        pairs.append((w_ref.at[band, at], out_ref.at[band, :]))
    run_copies(pairs, sems)


def hold(out_proj, target, tp_count):
    rows, columns = out_proj.shape[0], out_proj.shape[1] // tp_count
    return pl.pallas_call(
        hold_kernel,
        out_shape=jax.ShapeDtypeStruct((rows, columns), out_proj.dtype),
        grid_spec=pltpu.PrefetchScalarGridSpec(
            num_scalar_prefetch=1,
            grid=(),
            in_specs=[HBM],
            out_specs=VMEM,
            scratch_shapes=[pltpu.SemaphoreType.DMA((16,))],
        ),
        compiler_params=COPIES,
        cost_estimate=pl.CostEstimate(
            flops=0, bytes_accessed=4 * rows * columns, transcendentals=0
        ),
    )(target.reshape(1), out_proj)


def project_kernel(groups, *refs):
    ins, w_ref, out_ref = refs[:groups], refs[groups], refs[groups + 1]
    depth = ins[0].shape[1]
    columns = out_ref.shape[1]
    tile = columns // 4
    for i in range(4):
        at = slice(i * tile, (i + 1) * tile)
        acc = None
        for j in range(groups):
            row = pl.multiple_of(lax.bitwise_xor(my_group(), j) * depth, depth)
            dot = jnp.dot(
                ins[j][...], w_ref[pl.ds(row, depth), at], preferred_element_type=jnp.float32
            )
            acc = dot if acc is None else acc + dot
        out_ref[:, at] = acc.astype(out_ref.dtype)


def project(parts, held, dtype):
    groups = len(parts)
    half = parts[0].shape[0]
    rows, columns = held.shape
    return pl.pallas_call(
        functools.partial(project_kernel, groups),
        out_shape=jax.ShapeDtypeStruct((half, columns), dtype),
        in_specs=[VMEM] * (groups + 1),
        out_specs=VMEM,
        compiler_params=PARAMS,
        cost_estimate=pl.CostEstimate(
            flops=2 * half * rows * columns,
            bytes_accessed=2 * rows * columns,
            transcendentals=0,
        ),
    )(*parts, held)


def finish_kernel(groups, *refs):
    parts_ref, mine_ref, other_ref = refs[:3]
    sums, out_ref = refs[3:-1], refs[-1]
    width = mine_ref.shape[2]
    depth = parts_ref.shape[2]
    half = out_ref.shape[0] // 2
    core = lax.rem(lax.axis_index("ctx"), 2)
    group = my_group()
    for j in range(groups):
        for which, ref in ((core, mine_ref), (1 - core, other_ref)):
            at = (2 * lax.bitwise_xor(group, j) + which) * width
            at = pl.ds(pl.multiple_of(at, width), width)
            for i in range(2):
                acc = None
                for array in sums[i * (len(sums) // 2) : (i + 1) * (len(sums) // 2)]:
                    here = array[:, at].astype(jnp.float32)
                    acc = here if acc is None else acc + here
                for m in range(groups):
                    row = pl.multiple_of(lax.bitwise_xor(group, m) * depth, depth)
                    acc = acc + jnp.dot(
                        parts_ref[i * groups + m],
                        ref[j, pl.ds(row, depth), :],
                        preferred_element_type=jnp.float32,
                    )
                out_ref[i * half : (i + 1) * half, at] = acc.astype(out_ref.dtype)


def finish(parts, mine, other, low, high, groups):
    half, columns = low[0].shape
    return pl.pallas_call(
        functools.partial(finish_kernel, groups),
        out_shape=jax.ShapeDtypeStruct((2 * half, columns), jnp.bfloat16),
        in_specs=[VMEM] * (3 + len(low) + len(high)),
        out_specs=VMEM,
        name="finish",
        compiler_params=PARAMS,
        cost_estimate=pl.CostEstimate(
            flops=4 * half * mine.shape[1] * columns, bytes_accessed=12 << 20, transcendentals=0
        ),
    )(parts, mine, other, *low, *high)


def exchange_body(queries, attn_keys, attn_values, out_proj):
    ctx_count, tp_count = lax.axis_size("ctx"), lax.axis_size("tp")
    z = lax.axis_index("tp")
    groups = ctx_count // 2
    half = queries.shape[0] // 2
    width = queries.shape[1] // groups
    f32, bf16 = jnp.float32, jnp.bfloat16
    others = range(groups - 1, 0, -1)
    ends = [(0, 1), (tp_count - 1, tp_count - 2)]

    def swap(arrays):
        got = {0: arrays[0]}
        for j in others:
            pairs = [(d, d ^ (2 * j)) for d in range(ctx_count)]
            got[j] = lax.ppermute(arrays[j], "ctx", pairs)
        return [got[j] for j in range(groups)]

    def pair_swap(array):
        return lax.ppermute(array, "ctx", [(d, d ^ 1) for d in range(ctx_count)])

    def tokens(row0):
        packed = pack(queries, attn_keys, attn_values, row0, half, groups)
        return swap(packed)

    def paired(own):
        stacked = jnp.stack([array[1:] for array in own])
        return own, pair_swap(stacked)

    def attended(phase_inputs):
        outs = attention(phase_inputs, groups, half, width)
        return swap(outs)

    out_proj = pltpu.with_memory_space_constraint(out_proj, pltpu.HBM)
    queries = pltpu.with_memory_space_constraint(queries, pltpu.HBM)
    attn_keys = pltpu.with_memory_space_constraint(attn_keys, pltpu.HBM)
    attn_values = pltpu.with_memory_space_constraint(attn_values, pltpu.HBM)
    low = tokens(0)
    share = piece(out_proj, tp_count, ctx_count)
    share = lax.ppermute(share, "tp", ends)
    lower = z < tp_count // 2
    held = {}
    for t in range(tp_count - 1, tp_count // 2 - 1, -1):
        held[f"a{t}"] = jnp.where(lower, t, tp_count - 1 - t)
    for t in range(tp_count - 1, tp_count // 2, -1):
        held[f"b{t}"] = jnp.where(lower, tp_count - 1 - t, t)
    held["own"] = z
    for tag in held:
        held[tag] = hold(out_proj, held[tag].astype(jnp.int32), tp_count)

    low = paired(low)
    parts_low = attended([low])
    high = paired(tokens(half))
    parts_high = attended([low, high])

    share = swap([share] * groups)
    mine = jnp.stack(share)
    other = pair_swap(mine)

    def line(parts):
        chunks = {}
        for tag in held:
            chunks[tag] = project(parts, held[tag], f32)
        last = [chunks["own"]]
        for t in range(tp_count - 1, 1, -1):
            arrived = None
            for l in range(t):
                send = chunks[f"a{t}" if 2 * l < tp_count else f"b{t}"]
                if arrived is not None:
                    send = send + arrived.astype(f32)
                send = send.astype(bf16)
                pairs = [(l, l + 1), (tp_count - 1 - l, tp_count - 2 - l)]
                arrived = lax.ppermute(send, "tp", pairs)
            last.append(arrived)
        return last

    low_sums = line(parts_low)
    high_sums = line(parts_high)
    near = lax.ppermute(jnp.stack(parts_low + parts_high), "tp", ends)
    return finish(near, mine, other, low_sums, high_sums, groups)


def body(queries, attn_keys, attn_values, out_proj):
    ctx_count, tp_count = lax.axis_size("ctx"), lax.axis_size("tp")
    heads_local = queries.shape[1] // HS
    groups = ctx_count // 2
    paired = ctx_count % 2 == 0 and groups > 1 and groups & (groups - 1) == 0
    if paired and heads_local % groups == 0 and tp_count > 3 and tp_count % 2 == 0:
        return exchange_body(queries, attn_keys, attn_values, out_proj)
    return general_body(queries, attn_keys, attn_values, out_proj)


def solution(mesh):
    in_specs = (P("ctx", "tp"), P("ctx", "tp"), P("ctx", "tp"), P("tp", None))
    out_specs = P("ctx", "tp")
    return jax.shard_map(body, mesh=mesh, in_specs=in_specs, out_specs=out_specs, check_vma=False)
```

```python
import functools
import math

import jax
import jax.numpy as jnp
from jax import lax
from jax.experimental import pallas as pl
from jax.experimental.pallas import tpu as pltpu
from jax.sharding import PartitionSpec as P


HS = 128
ANY = pl.BlockSpec(memory_space=pl.ANY)
HBM = pl.BlockSpec(memory_space=pltpu.HBM)
VMEM = pl.BlockSpec(memory_space=pltpu.VMEM)
COPIES = pltpu.CompilerParams(vmem_limit_bytes=1 << 20)
PARAMS = pltpu.CompilerParams(vmem_limit_bytes=8 << 20)


def gathered_attention(queries, attn_keys, attn_values):
    ctx_count = lax.axis_size("ctx")
    ctx_index = lax.axis_index("ctx")
    tok_dev = queries.shape[0]
    half_len = tok_dev // 2
    heads_local = queries.shape[1] // HS
    query_heads = queries.reshape(tok_dev, heads_local, HS)
    offsets = jnp.arange(half_len, dtype=jnp.int32)
    query_pos = jnp.concatenate(
        [ctx_index * half_len + offsets, (2 * ctx_count - 1 - ctx_index) * half_len + offsets]
    )
    key_heads = lax.all_gather(attn_keys, "ctx", axis=0, tiled=True).reshape(-1, heads_local, HS)
    value_heads = lax.all_gather(attn_values, "ctx", axis=0, tiled=True).reshape(-1, heads_local, HS)
    stored = jnp.arange(key_heads.shape[0], dtype=jnp.int32)
    device = stored // tok_dev
    within = stored % tok_dev
    key_pos = jnp.where(
        within < half_len,
        device * half_len + within,
        (2 * ctx_count - 1 - device) * half_len + within - half_len,
    )
    scores = jnp.einsum("rhd,phd->hrp", query_heads, key_heads, preferred_element_type=jnp.float32)
    scores = scores * (1.0 / HS**0.5)
    visible = key_pos[None, None, :] <= query_pos[None, :, None]
    scores = jnp.where(visible, scores, -1e30)
    top = jnp.max(scores, axis=2, keepdims=True)
    weights = jnp.where(visible, jnp.exp(scores - top), 0.0)
    total = jnp.sum(weights, axis=2)
    update = jnp.einsum(
        "hrp,phd->rhd", weights.astype(jnp.bfloat16), value_heads, preferred_element_type=jnp.float32
    )
    attended = update / jnp.transpose(total)[:, :, None]
    return attended.reshape(tok_dev, heads_local * HS).astype(jnp.bfloat16)


def general_body(queries, attn_keys, attn_values, out_proj):
    attended = gathered_attention(queries, attn_keys, attn_values)
    partial_value = jnp.dot(attended, out_proj, preferred_element_type=jnp.float32).astype(
        jnp.bfloat16
    )
    return lax.psum_scatter(partial_value, "tp", scatter_dimension=1, tiled=True)


def my_group():
    return lax.axis_index("ctx") // 2


def run_copies(pairs, sems):
    copies = [pltpu.make_async_copy(src, dst, sems.at[i]) for i, (src, dst) in enumerate(pairs)]
    for copy in copies:
        copy.start()
    for copy in copies:
        copy.wait()


def pack_kernel(row0, q_ref, k_ref, v_ref, *rest):
    outs, sems = rest[:-1], rest[-1]
    half, width = outs[0].shape[1:]
    pairs = []
    for j, out in enumerate(outs):
        column = pl.multiple_of(lax.bitwise_xor(my_group(), j) * width, width)
        for i, ref in enumerate((q_ref, k_ref, v_ref)):
            pairs.append((ref.at[pl.ds(row0, half), pl.ds(column, width)], out.at[i]))
    run_copies(pairs, sems)


def pack(queries, attn_keys, attn_values, row0, half, groups):
    width = queries.shape[1] // groups
    out = jax.ShapeDtypeStruct((3, half, width), queries.dtype)
    return pl.pallas_call(
        functools.partial(pack_kernel, row0),
        out_shape=[out] * groups,
        in_specs=[HBM] * 3,
        out_specs=[VMEM] * groups,
        scratch_shapes=[pltpu.SemaphoreType.DMA((3 * groups,))],
        compiler_params=COPIES,
        cost_estimate=pl.CostEstimate(
            flops=0, bytes_accessed=6 * half * width * groups * 2, transcendentals=0
        ),
    )(queries, attn_keys, attn_values)


def piece_kernel(tp_count, w_ref, out_ref, sems):
    width = out_ref.shape[1]
    z = lax.axis_index("tp")
    target = jnp.where(z == 0, 1, tp_count - 2)
    column = target * (w_ref.shape[1] // tp_count) + lax.axis_index("ctx") * width
    column = pl.multiple_of(column, width)
    run_copies([(w_ref.at[:, pl.ds(column, width)], out_ref)], sems)


def piece(out_proj, tp_count, ctx_count):
    width = out_proj.shape[1] // tp_count // ctx_count
    return pl.pallas_call(
        functools.partial(piece_kernel, tp_count),
        out_shape=jax.ShapeDtypeStruct((out_proj.shape[0], width), out_proj.dtype),
        in_specs=[HBM],
        out_specs=VMEM,
        scratch_shapes=[pltpu.SemaphoreType.DMA((1,))],
        name="piece",
        compiler_params=COPIES,
        cost_estimate=pl.CostEstimate(
            flops=0, bytes_accessed=4 * out_proj.shape[0] * width, transcendentals=0
        ),
    )(out_proj)


def attend(groups, phases, group, core, ins, outs):
    half, width = outs[0].shape
    rate = math.log2(math.e) / HS**0.5
    per_phase = 2 * groups
    row = lax.broadcasted_iota(jnp.int32, (half, 2 * half), 0)
    col = lax.broadcasted_iota(jnp.int32, (half, 2 * half), 1)
    other_seen = core == (1 if phases == 1 else 0)
    visible = col < jnp.where(other_seen, 2 * half, half)
    visible = visible & ((col >= half) | (col <= row))
    contract = (((1,), (1,)), ((), ()))
    every = list(range(groups))

    tiles = []
    for phase in range(phases):
        for at in every:
            if phase < phases - 1:
                tiles.append((phase, at, every))
            elif phases == 1:
                tiles.append((phase, at, every[at:]))
            else:
                tiles.append((phase, at, every[: at + 1]))

    def keys_of(phase, at, which, lanes):
        own = ins[phase * per_phase + (at ^ group)]
        other = ins[phase * per_phase + groups + (at ^ group)]
        return jnp.concatenate([own[which, :, lanes], other[which, :, lanes]], axis=0)

    def rows(array, i):
        return array[i * half : (i + 1) * half]

    for head in range(width // HS):
        lanes = slice(head * HS, (head + 1) * HS)
        query = {
            at: ins[(phases - 1) * per_phase + (at ^ group)][0, :, lanes] for at in every
        }
        scores, best, total, acc = {}, {}, {}, {}
        for phase, at, seen in tiles:
            tall = jnp.concatenate([query[a] for a in seen], axis=0)
            dot = lax.dot_general(
                tall, keys_of(phase, at, 1, lanes), contract, preferred_element_type=jnp.float32
            )
            for i, a in enumerate(seen):
                mine = rows(dot, i)
                if a == at and phase == phases - 1:
                    mine = jnp.where(visible, mine, -1e30)
                scores[phase, at, a] = mine
                best[a] = jnp.maximum(best[a], mine) if a in best else mine
        top = {a: jnp.max(best[a], axis=1, keepdims=True) for a in every}
        for phase, at, seen in tiles:
            weights = []
            for a in seen:
                mine = jnp.exp2((scores[phase, at, a] - top[a]) * rate)
                total[a] = total[a] + mine if a in total else mine
                weights.append(mine.astype(jnp.bfloat16))
            dot = jnp.dot(
                jnp.concatenate(weights, axis=0),
                keys_of(phase, at, 2, lanes),
                preferred_element_type=jnp.float32,
            )
            for i, a in enumerate(seen):
                mine = rows(dot, i)
                acc[a] = acc[a] + mine if a in acc else mine
        for a in every:
            out = acc[a] / jnp.sum(total[a], axis=1, keepdims=True)
            outs[a ^ group][:, lanes] = out.astype(outs[0].dtype)


def attention_kernel(groups, phases, *refs):
    ins, outs = refs[:-groups], refs[-groups:]
    core = lax.rem(lax.axis_index("ctx"), 2)
    for group in range(groups):

        @pl.when(my_group() == group)
        def _(group=group):
            attend(groups, phases, group, core, ins, outs)


def attention(phase_inputs, groups, half, width):
    phases = len(phase_inputs)
    flat = [array for own, other in phase_inputs for array in (*own, *other)]
    out = jax.ShapeDtypeStruct((half, width), jnp.bfloat16)
    elements = groups * width // HS * half * half * (groups + 1 if phases == 1 else 3 * groups + 1)
    return pl.pallas_call(
        functools.partial(attention_kernel, groups, phases),
        out_shape=[out] * groups,
        in_specs=[VMEM] * len(flat),
        out_specs=[VMEM] * groups,
        compiler_params=PARAMS,
        cost_estimate=pl.CostEstimate(
            flops=4 * HS * elements, bytes_accessed=2 << 20, transcendentals=elements
        ),
    )(*flat)


def hold_kernel(place_ref, w_ref, out_ref, sems):
    columns, count = out_ref.shape[1], sems.shape[0]
    rows = out_ref.shape[0] // count
    at = pl.ds(pl.multiple_of(place_ref[0] * columns, columns), columns)
    pairs = []
    for i in range(count):
        band = pl.ds(i * rows, rows)
        pairs.append((w_ref.at[band, at], out_ref.at[band, :]))
    run_copies(pairs, sems)


def hold(out_proj, target, tp_count):
    rows, columns = out_proj.shape[0], out_proj.shape[1] // tp_count
    return pl.pallas_call(
        hold_kernel,
        out_shape=jax.ShapeDtypeStruct((rows, columns), out_proj.dtype),
        grid_spec=pltpu.PrefetchScalarGridSpec(
            num_scalar_prefetch=1,
            grid=(),
            in_specs=[HBM],
            out_specs=VMEM,
            scratch_shapes=[pltpu.SemaphoreType.DMA((16,))],
        ),
        compiler_params=COPIES,
        cost_estimate=pl.CostEstimate(
            flops=0, bytes_accessed=4 * rows * columns, transcendentals=0
        ),
    )(target.reshape(1), out_proj)


def project_kernel(groups, *refs):
    ins, w_ref, out_ref = refs[:groups], refs[groups], refs[groups + 1]
    depth = ins[0].shape[1]
    columns = out_ref.shape[1]
    tile = columns // 4
    for i in range(4):
        at = slice(i * tile, (i + 1) * tile)
        acc = None
        for j in range(groups):
            row = pl.multiple_of(lax.bitwise_xor(my_group(), j) * depth, depth)
            dot = jnp.dot(
                ins[j][...], w_ref[pl.ds(row, depth), at], preferred_element_type=jnp.float32
            )
            acc = dot if acc is None else acc + dot
        out_ref[:, at] = acc.astype(out_ref.dtype)


def project(parts, held, dtype):
    groups = len(parts)
    half = parts[0].shape[0]
    rows, columns = held.shape
    return pl.pallas_call(
        functools.partial(project_kernel, groups),
        out_shape=jax.ShapeDtypeStruct((half, columns), dtype),
        in_specs=[VMEM] * (groups + 1),
        out_specs=VMEM,
        compiler_params=PARAMS,
        cost_estimate=pl.CostEstimate(
            flops=2 * half * rows * columns,
            bytes_accessed=2 * rows * columns,
            transcendentals=0,
        ),
    )(*parts, held)


def near_kernel(groups, *refs):
    parts_ref, mine, other = refs[0], refs[1 : groups + 1], refs[groups + 1 : 2 * groups + 1]
    sums, outs = refs[2 * groups + 1 : -2], refs[-2:]
    width = mine[0].shape[1]
    depth = parts_ref.shape[2]
    core = lax.rem(lax.axis_index("ctx"), 2)
    group = my_group()
    for j in range(groups):
        for which, ref in ((core, mine[j]), (1 - core, other[j])):
            at = (2 * lax.bitwise_xor(group, j) + which) * width
            at = pl.ds(pl.multiple_of(at, width), width)
            for i, out_ref in enumerate(outs):
                acc = sums[i][:, at].astype(jnp.float32)
                for array in sums[2:] if i == 0 else ():
                    acc = acc + array[:, at].astype(jnp.float32)
                for m in range(groups):
                    row = pl.multiple_of(lax.bitwise_xor(group, m) * depth, depth)
                    acc = acc + jnp.dot(
                        parts_ref[i * groups + m],
                        ref[pl.ds(row, depth), :],
                        preferred_element_type=jnp.float32,
                    )
                out_ref[:, at] = acc.astype(out_ref.dtype)


def near_sums(parts, mine, other, low, high, groups):
    half, columns = low[0].shape
    return pl.pallas_call(
        functools.partial(near_kernel, groups),
        out_shape=[
            jax.ShapeDtypeStruct((half, columns), jnp.bfloat16),
            jax.ShapeDtypeStruct((half, columns), jnp.float32),
        ],
        in_specs=[VMEM] * (2 * groups + 2 + len(low)),
        out_specs=[VMEM] * 2,
        name="nsum",
        compiler_params=PARAMS,
        cost_estimate=pl.CostEstimate(
            flops=4 * half * mine[0].shape[0] * columns, bytes_accessed=12 << 20, transcendentals=0
        ),
    )(parts, *mine, *other, low[0], high, *low[1:])


def finish_kernel(low_ref, high_ref, *refs):
    arrived, out_ref, made, sems = refs[:-3], refs[-3], refs[-2], refs[-1]
    half, columns = made.shape
    count = sems.shape[0] - 1
    tile = columns // count
    copies = [pltpu.make_async_copy(low_ref, out_ref.at[pl.ds(0, half), :], sems.at[count])]
    copies[0].start()
    for i in range(count):
        at = pl.ds(i * tile, tile)
        acc = high_ref[:, at]
        for ref in arrived:
            acc = acc + ref[:, at].astype(jnp.float32)
        made[:, at] = acc.astype(made.dtype)
        copy = pltpu.make_async_copy(
            made.at[:, at], out_ref.at[pl.ds(half, half), at], sems.at[i]
        )
        copy.start()
        copies.append(copy)
    for copy in copies:
        copy.wait()


def finish(low, high, arrived):
    half, columns = low.shape
    return pl.pallas_call(
        finish_kernel,
        out_shape=jax.ShapeDtypeStruct((2 * half, columns), jnp.bfloat16),
        in_specs=[VMEM] * (2 + len(arrived)),
        out_specs=HBM,
        scratch_shapes=[
            pltpu.VMEM((half, columns), jnp.bfloat16),
            pltpu.SemaphoreType.DMA((5,)),
        ],
        name="finish",
        compiler_params=PARAMS,
        cost_estimate=pl.CostEstimate(
            flops=3 * half * columns, bytes_accessed=10 * half * columns, transcendentals=0
        ),
    )(low, high, *arrived)


def exchange_body(queries, attn_keys, attn_values, out_proj):
    ctx_count, tp_count = lax.axis_size("ctx"), lax.axis_size("tp")
    z = lax.axis_index("tp")
    groups = ctx_count // 2
    half = queries.shape[0] // 2
    width = queries.shape[1] // groups
    f32, bf16 = jnp.float32, jnp.bfloat16
    others = range(groups - 1, 0, -1)
    ends = [(0, 1), (tp_count - 1, tp_count - 2)]

    def swap(arrays):
        got = {0: arrays[0]}
        for j in others:
            pairs = [(d, d ^ (2 * j)) for d in range(ctx_count)]
            got[j] = lax.ppermute(arrays[j], "ctx", pairs)
        return [got[j] for j in range(groups)]

    def pair_swap(array):
        return lax.ppermute(array, "ctx", [(d, d ^ 1) for d in range(ctx_count)])

    def tokens(row0):
        packed = pack(queries, attn_keys, attn_values, row0, half, groups)
        return swap(packed)

    def paired(own):
        return own, [pair_swap(own[j]) for j in range(groups)]

    def attended(phase_inputs):
        outs = attention(phase_inputs, groups, half, width)
        return swap(outs)

    out_proj = pltpu.with_memory_space_constraint(out_proj, pltpu.HBM)
    queries = pltpu.with_memory_space_constraint(queries, pltpu.HBM)
    attn_keys = pltpu.with_memory_space_constraint(attn_keys, pltpu.HBM)
    attn_values = pltpu.with_memory_space_constraint(attn_values, pltpu.HBM)
    low = tokens(0)
    share = piece(out_proj, tp_count, ctx_count)
    share = lax.ppermute(share, "tp", ends)
    lower = z < tp_count // 2
    held = {}
    for t in range(tp_count - 1, tp_count // 2 - 1, -1):
        held[f"a{t}"] = jnp.where(lower, t, tp_count - 1 - t)
    for t in range(tp_count - 1, tp_count // 2, -1):
        held[f"b{t}"] = jnp.where(lower, tp_count - 1 - t, t)
    held["own"] = z
    for tag in held:
        held[tag] = hold(out_proj, held[tag].astype(jnp.int32), tp_count)

    low = paired(low)
    parts_low = attended([low])
    high = paired(tokens(half))
    parts_high = attended([low, high])

    share = swap([share] * groups)
    mine, other = paired(share)

    def line(parts):
        chunks = {}
        for tag in held:
            chunks[tag] = project(parts, held[tag], bf16)
        last = [chunks["own"]]
        for t in range(tp_count - 1, 1, -1):
            arrived = None
            for l in range(t):
                send = chunks[f"a{t}" if 2 * l < tp_count else f"b{t}"]
                if arrived is not None:
                    send = (send.astype(f32) + arrived.astype(f32)).astype(bf16)
                pairs = [(l, l + 1), (tp_count - 1 - l, tp_count - 2 - l)]
                arrived = lax.ppermute(send, "tp", pairs)
            last.append(arrived)
        return last

    low_sums = line(parts_low)
    high_sums = line(parts_high)
    near = lax.ppermute(jnp.stack(parts_low + parts_high), "tp", ends)
    low_rows, high_rows = near_sums(near, mine, other, low_sums, high_sums[0], groups)
    return finish(low_rows, high_rows, high_sums[1:])


def body(queries, attn_keys, attn_values, out_proj):
    ctx_count, tp_count = lax.axis_size("ctx"), lax.axis_size("tp")
    heads_local = queries.shape[1] // HS
    groups = ctx_count // 2
    paired = ctx_count % 2 == 0 and groups > 1 and groups & (groups - 1) == 0
    if paired and heads_local % groups == 0 and tp_count > 3 and tp_count % 2 == 0:
        return exchange_body(queries, attn_keys, attn_values, out_proj)
    return general_body(queries, attn_keys, attn_values, out_proj)


def solution(mesh):
    in_specs = (P("ctx", "tp"), P("ctx", "tp"), P("ctx", "tp"), P("tp", None))
    out_specs = P("ctx", "tp")
    return jax.shard_map(body, mesh=mesh, in_specs=in_specs, out_specs=out_specs, check_vma=False)
```

```python
import functools
import math

import jax
import jax.numpy as jnp
from jax import lax
from jax.experimental import pallas as pl
from jax.experimental.pallas import tpu as pltpu
from jax.sharding import PartitionSpec as P


HS = 128
ANY = pl.BlockSpec(memory_space=pl.ANY)
HBM = pl.BlockSpec(memory_space=pltpu.HBM)
VMEM = pl.BlockSpec(memory_space=pltpu.VMEM)
COPIES = pltpu.CompilerParams(vmem_limit_bytes=1 << 20)
PARAMS = pltpu.CompilerParams(vmem_limit_bytes=8 << 20)


def gathered_attention(queries, attn_keys, attn_values):
    ctx_count = lax.axis_size("ctx")
    ctx_index = lax.axis_index("ctx")
    tok_dev = queries.shape[0]
    half_len = tok_dev // 2
    heads_local = queries.shape[1] // HS
    query_heads = queries.reshape(tok_dev, heads_local, HS)
    offsets = jnp.arange(half_len, dtype=jnp.int32)
    query_pos = jnp.concatenate(
        [ctx_index * half_len + offsets, (2 * ctx_count - 1 - ctx_index) * half_len + offsets]
    )
    key_heads = lax.all_gather(attn_keys, "ctx", axis=0, tiled=True).reshape(-1, heads_local, HS)
    value_heads = lax.all_gather(attn_values, "ctx", axis=0, tiled=True).reshape(-1, heads_local, HS)
    stored = jnp.arange(key_heads.shape[0], dtype=jnp.int32)
    device = stored // tok_dev
    within = stored % tok_dev
    key_pos = jnp.where(
        within < half_len,
        device * half_len + within,
        (2 * ctx_count - 1 - device) * half_len + within - half_len,
    )
    scores = jnp.einsum("rhd,phd->hrp", query_heads, key_heads, preferred_element_type=jnp.float32)
    scores = scores * (1.0 / HS**0.5)
    visible = key_pos[None, None, :] <= query_pos[None, :, None]
    scores = jnp.where(visible, scores, -1e30)
    top = jnp.max(scores, axis=2, keepdims=True)
    weights = jnp.where(visible, jnp.exp(scores - top), 0.0)
    total = jnp.sum(weights, axis=2)
    update = jnp.einsum(
        "hrp,phd->rhd", weights.astype(jnp.bfloat16), value_heads, preferred_element_type=jnp.float32
    )
    attended = update / jnp.transpose(total)[:, :, None]
    return attended.reshape(tok_dev, heads_local * HS).astype(jnp.bfloat16)


def general_body(queries, attn_keys, attn_values, out_proj):
    attended = gathered_attention(queries, attn_keys, attn_values)
    partial_value = jnp.dot(attended, out_proj, preferred_element_type=jnp.float32).astype(
        jnp.bfloat16
    )
    return lax.psum_scatter(partial_value, "tp", scatter_dimension=1, tiled=True)


def my_group():
    return lax.axis_index("ctx") // 2


def run_copies(pairs, sems):
    copies = [pltpu.make_async_copy(src, dst, sems.at[i]) for i, (src, dst) in enumerate(pairs)]
    for copy in copies:
        copy.start()
    for copy in copies:
        copy.wait()


def pack_kernel(row0, q_ref, k_ref, v_ref, *rest):
    outs, sems = rest[:-1], rest[-1]
    half, width = outs[0].shape[1:]
    pairs = []
    for j, out in enumerate(outs):
        column = pl.multiple_of(lax.bitwise_xor(my_group(), j) * width, width)
        for i, ref in enumerate((q_ref, k_ref, v_ref)):
            pairs.append((ref.at[pl.ds(row0, half), pl.ds(column, width)], out.at[i]))
    run_copies(pairs, sems)


def pack(queries, attn_keys, attn_values, row0, half, groups):
    width = queries.shape[1] // groups
    out = jax.ShapeDtypeStruct((3, half, width), queries.dtype)
    return pl.pallas_call(
        functools.partial(pack_kernel, row0),
        out_shape=[out] * groups,
        in_specs=[HBM] * 3,
        out_specs=[VMEM] * groups,
        scratch_shapes=[pltpu.SemaphoreType.DMA((3 * groups,))],
        compiler_params=COPIES,
        cost_estimate=pl.CostEstimate(
            flops=0, bytes_accessed=6 * half * width * groups * 2, transcendentals=0
        ),
    )(queries, attn_keys, attn_values)


def piece_kernel(tp_count, w_ref, out_ref, sems):
    width = out_ref.shape[1]
    z = lax.axis_index("tp")
    target = jnp.where(z == 0, 1, tp_count - 2)
    column = target * (w_ref.shape[1] // tp_count) + lax.axis_index("ctx") * width
    column = pl.multiple_of(column, width)
    run_copies([(w_ref.at[:, pl.ds(column, width)], out_ref)], sems)


def piece(out_proj, tp_count, ctx_count):
    width = out_proj.shape[1] // tp_count // ctx_count
    return pl.pallas_call(
        functools.partial(piece_kernel, tp_count),
        out_shape=jax.ShapeDtypeStruct((out_proj.shape[0], width), out_proj.dtype),
        in_specs=[HBM],
        out_specs=VMEM,
        scratch_shapes=[pltpu.SemaphoreType.DMA((1,))],
        name="piece",
        compiler_params=COPIES,
        cost_estimate=pl.CostEstimate(
            flops=0, bytes_accessed=4 * out_proj.shape[0] * width, transcendentals=0
        ),
    )(out_proj)


def attend(groups, phases, group, core, ins, outs):
    half, width = outs[0].shape
    rate = math.log2(math.e) / HS**0.5
    per_phase = 2 * groups
    row = lax.broadcasted_iota(jnp.int32, (half, 2 * half), 0)
    col = lax.broadcasted_iota(jnp.int32, (half, 2 * half), 1)
    other_seen = core == (1 if phases == 1 else 0)
    visible = col < jnp.where(other_seen, 2 * half, half)
    visible = visible & ((col >= half) | (col <= row))
    contract = (((1,), (1,)), ((), ()))
    every = list(range(groups))

    tiles = []
    for phase in range(phases):
        for at in every:
            if phase < phases - 1:
                tiles.append((phase, at, every))
            elif phases == 1:
                tiles.append((phase, at, every[at:]))
            else:
                tiles.append((phase, at, every[: at + 1]))

    def keys_of(phase, at, which, lanes):
        own = ins[phase * per_phase + (at ^ group)]
        other = ins[phase * per_phase + groups + (at ^ group)]
        return jnp.concatenate([own[which, :, lanes], other[which, :, lanes]], axis=0)

    def rows(array, i):
        return array[i * half : (i + 1) * half]

    for head in range(width // HS):
        lanes = slice(head * HS, (head + 1) * HS)
        query = {
            at: ins[(phases - 1) * per_phase + (at ^ group)][0, :, lanes] for at in every
        }
        scores, best, total, acc = {}, {}, {}, {}
        for phase, at, seen in tiles:
            tall = jnp.concatenate([query[a] for a in seen], axis=0)
            dot = lax.dot_general(
                tall, keys_of(phase, at, 1, lanes), contract, preferred_element_type=jnp.float32
            )
            for i, a in enumerate(seen):
                mine = rows(dot, i)
                if a == at and phase == phases - 1:
                    mine = jnp.where(visible, mine, -1e30)
                scores[phase, at, a] = mine
                best[a] = jnp.maximum(best[a], mine) if a in best else mine
        top = {a: jnp.max(best[a], axis=1, keepdims=True) for a in every}
        for phase, at, seen in tiles:
            weights = []
            for a in seen:
                mine = jnp.exp2((scores[phase, at, a] - top[a]) * rate)
                total[a] = total[a] + mine if a in total else mine
                weights.append(mine.astype(jnp.bfloat16))
            dot = jnp.dot(
                jnp.concatenate(weights, axis=0),
                keys_of(phase, at, 2, lanes),
                preferred_element_type=jnp.float32,
            )
            for i, a in enumerate(seen):
                mine = rows(dot, i)
                acc[a] = acc[a] + mine if a in acc else mine
        for a in every:
            out = acc[a] / jnp.sum(total[a], axis=1, keepdims=True)
            outs[a ^ group][:, lanes] = out.astype(outs[0].dtype)


def attention_kernel(groups, phases, *refs):
    ins, outs = refs[:-groups], refs[-groups:]
    core = lax.rem(lax.axis_index("ctx"), 2)
    for group in range(groups):

        @pl.when(my_group() == group)
        def _(group=group):
            attend(groups, phases, group, core, ins, outs)


def attention(phase_inputs, groups, half, width):
    phases = len(phase_inputs)
    flat = [array for own, other in phase_inputs for array in (*own, *other)]
    out = jax.ShapeDtypeStruct((half, width), jnp.bfloat16)
    elements = groups * width // HS * half * half * (groups + 1 if phases == 1 else 3 * groups + 1)
    return pl.pallas_call(
        functools.partial(attention_kernel, groups, phases),
        out_shape=[out] * groups,
        in_specs=[VMEM] * len(flat),
        out_specs=[VMEM] * groups,
        compiler_params=PARAMS,
        cost_estimate=pl.CostEstimate(
            flops=4 * HS * elements, bytes_accessed=2 << 20, transcendentals=elements
        ),
    )(*flat)


def hold_kernel(place_ref, w_ref, out_ref, sems):
    columns, count = out_ref.shape[1], sems.shape[0]
    rows = out_ref.shape[0] // count
    at = pl.ds(pl.multiple_of(place_ref[0] * columns, columns), columns)
    pairs = []
    for i in range(count):
        band = pl.ds(i * rows, rows)
        pairs.append((w_ref.at[band, at], out_ref.at[band, :]))
    run_copies(pairs, sems)


def hold(out_proj, target, tp_count):
    rows, columns = out_proj.shape[0], out_proj.shape[1] // tp_count
    return pl.pallas_call(
        hold_kernel,
        out_shape=jax.ShapeDtypeStruct((rows, columns), out_proj.dtype),
        grid_spec=pltpu.PrefetchScalarGridSpec(
            num_scalar_prefetch=1,
            grid=(),
            in_specs=[HBM],
            out_specs=VMEM,
            scratch_shapes=[pltpu.SemaphoreType.DMA((16,))],
        ),
        compiler_params=COPIES,
        cost_estimate=pl.CostEstimate(
            flops=0, bytes_accessed=4 * rows * columns, transcendentals=0
        ),
    )(target.reshape(1), out_proj)


def project_kernel(groups, *refs):
    ins, w_ref, out_ref = refs[:groups], refs[groups], refs[groups + 1]
    depth = ins[0].shape[1]
    columns = out_ref.shape[1]
    tile = columns // 4
    for i in range(4):
        at = slice(i * tile, (i + 1) * tile)
        acc = None
        for j in range(groups):
            row = pl.multiple_of(lax.bitwise_xor(my_group(), j) * depth, depth)
            dot = jnp.dot(
                ins[j][...], w_ref[pl.ds(row, depth), at], preferred_element_type=jnp.float32
            )
            acc = dot if acc is None else acc + dot
        out_ref[:, at] = acc.astype(out_ref.dtype)


def project(parts, held, dtype):
    groups = len(parts)
    half = parts[0].shape[0]
    rows, columns = held.shape
    return pl.pallas_call(
        functools.partial(project_kernel, groups),
        out_shape=jax.ShapeDtypeStruct((half, columns), dtype),
        in_specs=[VMEM] * (groups + 1),
        out_specs=VMEM,
        compiler_params=PARAMS,
        cost_estimate=pl.CostEstimate(
            flops=2 * half * rows * columns,
            bytes_accessed=2 * rows * columns,
            transcendentals=0,
        ),
    )(*parts, held)


def near_kernel(groups, *refs):
    parts_ref, mine, other = refs[0], refs[1 : groups + 1], refs[groups + 1 : 2 * groups + 1]
    sums, out_ref, high_ref, low_s, sem = refs[2 * groups + 1 : -4], *refs[-4:]
    outs = (low_s, high_ref)
    width = mine[0].shape[1]
    depth = parts_ref.shape[2]
    core = lax.rem(lax.axis_index("ctx"), 2)
    group = my_group()
    for j in range(groups):
        for which, ref in ((core, mine[j]), (1 - core, other[j])):
            at = (2 * lax.bitwise_xor(group, j) + which) * width
            at = pl.ds(pl.multiple_of(at, width), width)
            for i, into in enumerate(outs):
                acc = sums[i][:, at].astype(jnp.float32)
                for array in sums[2:] if i == 0 else ():
                    acc = acc + array[:, at].astype(jnp.float32)
                for m in range(groups):
                    row = pl.multiple_of(lax.bitwise_xor(group, m) * depth, depth)
                    acc = acc + jnp.dot(
                        parts_ref[i * groups + m],
                        ref[pl.ds(row, depth), :],
                        preferred_element_type=jnp.float32,
                    )
                into[:, at] = acc.astype(into.dtype)
    half = low_s.shape[0]
    copy = pltpu.make_async_copy(low_s, out_ref.at[pl.ds(0, half), :], sem)
    copy.start()
    copy.wait()


def near_sums(parts, mine, other, low, high, groups):
    half, columns = low[0].shape
    return pl.pallas_call(
        functools.partial(near_kernel, groups),
        out_shape=[
            jax.ShapeDtypeStruct((2 * half, columns), jnp.bfloat16),
            jax.ShapeDtypeStruct((half, columns), jnp.float32),
        ],
        scratch_shapes=[pltpu.VMEM((half, columns), jnp.bfloat16), pltpu.SemaphoreType.DMA],
        in_specs=[VMEM] * (2 * groups + 2 + len(low)),
        out_specs=[HBM, VMEM],
        name="nsum",
        compiler_params=PARAMS,
        cost_estimate=pl.CostEstimate(
            flops=4 * half * mine[0].shape[0] * columns, bytes_accessed=12 << 20, transcendentals=0
        ),
    )(parts, *mine, *other, low[0], high, *low[1:])


def finish_kernel(rows_ref, high_ref, *refs):
    arrived, out_ref, made, sems = refs[:-3], refs[-3], refs[-2], refs[-1]
    half, columns = made.shape
    count = sems.shape[0]
    tile = columns // count
    copies = []
    for i in range(count):
        at = pl.ds(i * tile, tile)
        acc = high_ref[:, at]
        for ref in arrived:
            acc = acc + ref[:, at].astype(jnp.float32)
        made[:, at] = acc.astype(made.dtype)
        copy = pltpu.make_async_copy(
            made.at[:, at], out_ref.at[pl.ds(half, half), at], sems.at[i]
        )
        copy.start()
        copies.append(copy)
    for copy in copies:
        copy.wait()


def finish(rows, high, arrived):
    half, columns = high.shape
    return pl.pallas_call(
        finish_kernel,
        out_shape=jax.ShapeDtypeStruct((2 * half, columns), jnp.bfloat16),
        in_specs=[HBM] + [VMEM] * (1 + len(arrived)),
        out_specs=HBM,
        scratch_shapes=[
            pltpu.VMEM((half, columns), jnp.bfloat16),
            pltpu.SemaphoreType.DMA((4,)),
        ],
        input_output_aliases={0: 0},
        name="finish",
        compiler_params=PARAMS,
        cost_estimate=pl.CostEstimate(
            flops=3 * half * columns, bytes_accessed=10 * half * columns, transcendentals=0
        ),
    )(rows, high, *arrived)


def exchange_body(queries, attn_keys, attn_values, out_proj):
    ctx_count, tp_count = lax.axis_size("ctx"), lax.axis_size("tp")
    z = lax.axis_index("tp")
    groups = ctx_count // 2
    half = queries.shape[0] // 2
    width = queries.shape[1] // groups
    f32, bf16 = jnp.float32, jnp.bfloat16
    others = range(groups - 1, 0, -1)
    ends = [(0, 1), (tp_count - 1, tp_count - 2)]

    def swap(arrays):
        got = {0: arrays[0]}
        for j in others:
            pairs = [(d, d ^ (2 * j)) for d in range(ctx_count)]
            got[j] = lax.ppermute(arrays[j], "ctx", pairs)
        return [got[j] for j in range(groups)]

    def pair_swap(array):
        return lax.ppermute(array, "ctx", [(d, d ^ 1) for d in range(ctx_count)])

    def tokens(row0):
        packed = pack(queries, attn_keys, attn_values, row0, half, groups)
        return swap(packed)

    def paired(own):
        return own, [pair_swap(own[j]) for j in range(groups)]

    def attended(phase_inputs):
        outs = attention(phase_inputs, groups, half, width)
        return swap(outs)

    out_proj = pltpu.with_memory_space_constraint(out_proj, pltpu.HBM)
    queries = pltpu.with_memory_space_constraint(queries, pltpu.HBM)
    attn_keys = pltpu.with_memory_space_constraint(attn_keys, pltpu.HBM)
    attn_values = pltpu.with_memory_space_constraint(attn_values, pltpu.HBM)
    low = tokens(0)
    share = piece(out_proj, tp_count, ctx_count)
    share = lax.ppermute(share, "tp", ends)
    lower = z < tp_count // 2
    held = {}
    for t in range(tp_count - 1, tp_count // 2 - 1, -1):
        held[f"a{t}"] = jnp.where(lower, t, tp_count - 1 - t)
    for t in range(tp_count - 1, tp_count // 2, -1):
        held[f"b{t}"] = jnp.where(lower, tp_count - 1 - t, t)
    held["own"] = z
    for tag in held:
        held[tag] = hold(out_proj, held[tag].astype(jnp.int32), tp_count)

    low = paired(low)
    parts_low = attended([low])
    high = paired(tokens(half))
    parts_high = attended([low, high])

    share = swap([share] * groups)
    mine, other = paired(share)

    def line(parts):
        chunks = {}
        for tag in held:
            chunks[tag] = project(parts, held[tag], bf16)
        last = [chunks["own"]]
        for t in range(tp_count - 1, 1, -1):
            arrived = None
            for l in range(t):
                send = chunks[f"a{t}" if 2 * l < tp_count else f"b{t}"]
                if arrived is not None:
                    send = (send.astype(f32) + arrived.astype(f32)).astype(bf16)
                pairs = [(l, l + 1), (tp_count - 1 - l, tp_count - 2 - l)]
                arrived = lax.ppermute(send, "tp", pairs)
            last.append(arrived)
        return last

    low_sums = line(parts_low)
    high_sums = line(parts_high)
    near = lax.ppermute(jnp.stack(parts_low + parts_high), "tp", ends)
    low_rows, high_rows = near_sums(near, mine, other, low_sums, high_sums[0], groups)
    return finish(low_rows, high_rows, high_sums[1:])


def body(queries, attn_keys, attn_values, out_proj):
    ctx_count, tp_count = lax.axis_size("ctx"), lax.axis_size("tp")
    heads_local = queries.shape[1] // HS
    groups = ctx_count // 2
    paired = ctx_count % 2 == 0 and groups > 1 and groups & (groups - 1) == 0
    if paired and heads_local % groups == 0 and tp_count > 3 and tp_count % 2 == 0:
        return exchange_body(queries, attn_keys, attn_values, out_proj)
    return general_body(queries, attn_keys, attn_values, out_proj)


def solution(mesh):
    in_specs = (P("ctx", "tp"), P("ctx", "tp"), P("ctx", "tp"), P("tp", None))
    out_specs = P("ctx", "tp")
    return jax.shard_map(body, mesh=mesh, in_specs=in_specs, out_specs=out_specs, check_vma=False)
```
